32 devices in a mesh: adapter: 8 (over z, x), feature: 4 (over y, core).
Axes of the slice: x: 2, y: 2, z: 4, core: 2. Of those that a mesh axis runs over, the one named last changes fastest.
Arguments:
- adapter_down: bfloat16 [128, 16, 8192], P('adapter', None, 'feature'), may hold values from -6 to 6
- adapter_up: bfloat16 [128, 16, 8192], P('adapter', None, 'feature'), may hold values from -6 to 6
- fisher: float32 [128], P('adapter'), may hold values from 0.1 to 10
- init_v: float32 [8192, 64], P('feature'), may hold values from -0.0625 to 0.0625
- init_u: float32 [8192, 64], P('feature'), may hold values from -0.0625 to 0.0625
- prompt_rows: bfloat16 [4096, 8192], P('adapter', 'feature'), may hold values from -6 to 6
- request_ids: int32 [32], P('adapter'), may hold values from 0 to 127
Outputs:
- served: bfloat16 [4096, 8192], P('adapter', 'feature')
The draws below stay inside these ranges and needn't reach their ends.
All inputs are finite; a program needn't handle non-finite values.
Results may differ from the reference program's by a relative error of at most 0.025.
Values may be sent and summed in bfloat16 or wider, within the bound.
A program may use at most 64 MiB of HBM per device.

```python
import math
import jax
import jax.numpy as jnp
import numpy as np
from jax import lax

D = 8192
RANK = 16
BASIS = 64
SWEEPS = 3
BLOCK_ROWS = 128
ADAPTERS = 128
ROWS = 4096
BLOCKS = 32


def touch_ends(drawn, stream_key, low, top_value):
    longest = drawn.shape.index(max(drawn.shape))
    spots = []
    for shift in (0, 1):
        where = [jax.random.randint(jax.random.fold_in(stream_key, axis), (), 0, length) for axis, length in enumerate(drawn.shape)]
        where[longest] = (where[longest] + shift) % drawn.shape[longest]
        spots.append(tuple(where))
    return drawn.at[spots[0]].set(low).at[spots[1]].set(top_value)


def steps_of(rng, shape, split, smallest, top_value):
    def one(dim, shards_of):
        steps = jax.random.uniform(jax.random.fold_in(jax.random.fold_in(rng, 6), dim), (shards_of,), jnp.float32, smallest / len(split), top_value / len(split))
        return jnp.repeat(jnp.exp(steps), shape[dim] // shards_of).reshape((-1,) + (1,) * (len(shape) - dim - 1))

    level = one(*split[0])
    for cut in split[1:]:
        level = level * one(*cut)
    return level


def rank_bounds(number_of, skew):
    weights = [(1 << 20) // math.isqrt(grade ** skew) + 1 for grade in range(1, number_of + 1)]
    scale = 1 + sum(weights) // (1 << 30)
    return np.cumsum(np.array([max(1, weight // scale) for weight in weights]))


def ranked(stream_key, extent, number_of, slope):
    grid = rank_bounds(number_of, slope)
    lot = jax.random.randint(jax.random.fold_in(stream_key, 1), extent, 0, int(grid[number_of - 1]))
    grade = jnp.searchsorted(jnp.asarray(grid, jnp.int32), lot, side="right")
    return jax.random.permutation(jax.random.fold_in(stream_key, 2), number_of)[grade].astype(jnp.int32)


def gaussian(key, dims, scale, limit, shards=(), dtype=jnp.bfloat16):
    array = scale * jax.random.normal(key, dims, jnp.float32)
    if shards:
        array = array * steps_of(key, dims, shards, -0.22, 0.18)
    return jnp.clip(array, -limit, limit).astype(dtype)


def setup_inputs(seed: int = 0) -> dict:
    key_list = jax.random.split(jax.random.key(seed), 8)
    return {
        "adapter_down": gaussian(key_list[0], (ADAPTERS, RANK, D), 1.0, 6.0, ((0, 8), (2, 4))),
        "adapter_up": gaussian(key_list[1], (ADAPTERS, RANK, D), 1.0, 6.0, ((0, 8), (2, 4))),
        "fisher": jnp.clip(jnp.exp(math.log(10.0) - 4.6051702 * jax.random.uniform(key_list[2], (ADAPTERS,), jnp.float32) ** steps_of(key_list[2], (ADAPTERS,), ((0, 8),), -0.2, 0.2)), 0.1, 10.0),
        "init_v": gaussian(key_list[3], (D, BASIS), D ** -0.5, 0.0625, ((0, 4),), jnp.float32),
        "init_u": gaussian(key_list[4], (D, BASIS), D ** -0.5, 0.0625, ((0, 4),), jnp.float32),
        "prompt_rows": gaussian(key_list[5], (ROWS, D), 1.0, 6.0, ((0, 8), (1, 4))),
        "request_ids": touch_ends(ranked(key_list[6], (BLOCKS,), ADAPTERS, 2), jax.random.fold_in(key_list[6], 3), 0, ADAPTERS - 1).astype(jnp.int32),
    }


highest = lax.Precision.HIGHEST

def project(adapter_stack, basis_low):
    flat = adapter_stack.reshape(-1, adapter_stack.shape[-1])
    result = jnp.dot(flat.astype(jnp.float32), basis_low.astype(jnp.float32), preferred_element_type=jnp.float32)
    return result.reshape(adapter_stack.shape[0], adapter_stack.shape[1], -1)

def core_of(cols_q, rows_p):
    return jnp.einsum('irk,irl->ikl', cols_q, rows_p, precision=highest)

def numerator(adapter_stack, weighted):
    flat = adapter_stack.reshape(-1, adapter_stack.shape[-1])
    terms = weighted.reshape(-1, weighted.shape[-1])
    return lax.dot_general(flat.astype(jnp.float32), terms.astype(jnp.float32), (((0,), (0,)), ((), ())), preferred_element_type=jnp.float32)

def orthonormal(matrix):
    gram_sum = jnp.dot(matrix.T, matrix, precision=highest)
    factor = jnp.linalg.cholesky(gram_sum)
    return lax.linalg.triangular_solve(factor, matrix, left_side=False, lower=True, transpose_a=True)

def reference(adapter_down, adapter_up, fisher, init_v, init_u, prompt_rows, request_ids):
    basis_v = init_v
    basis_u = init_u
    weights = fisher[:, None, None]
    cols_q = project(adapter_up, basis_u.astype(jnp.bfloat16))
    for sweep_index in range(SWEEPS):
        rows_p = project(adapter_down, basis_v.astype(jnp.bfloat16))
        core_stack = core_of(cols_q, rows_p)
        weighted = (weights * jnp.einsum('irl,ikl->irk', rows_p, core_stack, precision=highest)).astype(jnp.bfloat16)
        basis_u = orthonormal(numerator(adapter_up, weighted))
        cols_q = project(adapter_up, basis_u.astype(jnp.bfloat16))
        core_stack = core_of(cols_q, rows_p)
        weighted = (weights * jnp.einsum('irk,ikl->irl', cols_q, core_stack, precision=highest)).astype(jnp.bfloat16)
        basis_v = orthonormal(numerator(adapter_down, weighted))
    rows_p = project(adapter_down, basis_v.astype(jnp.bfloat16))
    final_cores = core_of(cols_q, rows_p).astype(jnp.bfloat16)
    hidden = jnp.dot(prompt_rows.astype(jnp.float32), basis_v.astype(jnp.bfloat16).astype(jnp.float32), preferred_element_type=jnp.float32).astype(jnp.bfloat16)
    chosen = final_cores[request_ids.astype(jnp.int32)]
    blocked = hidden.reshape(BLOCKS, BLOCK_ROWS, BASIS)
    mixed_rows = jnp.einsum('bnl,bkl->bnk', blocked.astype(jnp.float32), chosen.astype(jnp.float32)).astype(jnp.bfloat16)
    served = jnp.dot(mixed_rows.reshape(ROWS, BASIS).astype(jnp.float32), basis_u.astype(jnp.bfloat16).T.astype(jnp.float32), preferred_element_type=jnp.float32)
    return served.astype(jnp.bfloat16)
```

```python
import functools
import math

import jax
import jax.numpy as jnp
from jax import lax
from jax.experimental import pallas as pl
from jax.experimental.pallas import tpu as pltpu
from jax.sharding import PartitionSpec as P

SWEEPS = 3
GROUP = 8
LANES = 128
MESH = pl.DeviceIdType.MESH
SEND = jnp.bfloat16

highest = lax.Precision.HIGHEST


def dot32(left, right):
    return jnp.dot(left, right, precision=highest, preferred_element_type=jnp.float32)


def dot_nt(left, right):
    return lax.dot_general(
        left, right, (((1,), (1,)), ((), ())), preferred_element_type=jnp.float32
    )


def inverse_factor(gram):
    width = gram.shape[0]
    rows = lax.broadcasted_iota(jnp.int32, (width, width), 0)
    columns = lax.broadcasted_iota(jnp.int32, (width, width), 1)
    eye = (rows == columns).astype(jnp.float32)
    table = jnp.concatenate([gram, eye], axis=1)
    blocks = [table[at : at + GROUP] for at in range(0, width, GROUP)]
    inner = lax.broadcasted_iota(jnp.int32, (GROUP, 1), 0)
    for k in range(width):
        first, offset = divmod(k, GROUP)
        row = blocks[first][offset : offset + 1]
        scaled = row / row[:, k : k + 1]
        for b in range(first, len(blocks)):
            factor = blocks[b][:, k : k + 1]
            if b == first:
                factor = jnp.where(inner > offset, factor, 0.0)
            blocks[b] = blocks[b] - factor * scaled
    table = jnp.concatenate(blocks, axis=0)
    pivots = jnp.sum(table[:, :width] * eye, axis=1, keepdims=True)
    return table[:, width:] / jnp.sqrt(pivots)


def weigh(rank, fresh, other, weights):
    total = fresh.shape[1]
    step = 128 if total % 128 == 0 and 128 % rank == 0 else total
    same = (
        lax.broadcasted_iota(jnp.int32, (step, step), 0) // rank
        == lax.broadcasted_iota(jnp.int32, (step, step), 1) // rank
    )
    parts = []
    for at in range(0, total, step):
        piece = fresh[:, at : at + step]
        inner = jnp.where(same, dot32(piece.T, piece), 0.0)
        parts.append(dot32(other[:, at : at + step], inner))
    joined = parts[0] if len(parts) == 1 else jnp.concatenate(parts, axis=1)
    return (joined * weights).astype(jnp.bfloat16)


def fold(square):
    half = square.shape[0] // 2
    return jnp.concatenate([square[:half], square[half:]], axis=1)


def unfold(packed):
    width = packed.shape[1] // 2
    return jnp.concatenate([packed[:, :width], packed[:, width:]], axis=0)


def kernel(
    na,
    nf,
    rank,
    down_ref,
    up_ref,
    prompt_ref,
    init_v_ref,
    init_u_ref,
    weights_ref,
    ids_ref,
    mixed_ref,
    basis_ref,
    flat,
    prompt,
    factors,
    part,
    arrived,
    numerator,
    proj_out,
    gram_out,
    proj_in,
    gram_in,
    init_out,
    init_in,
    hidden_out,
    hidden_in,
    all_q,
    all_p,
    load_sem,
    prompt_sem,
    scatter_sem,
    gather_sem,
    proj_sem,
    gram_sem,
    init_sem,
    hidden_sem,
    q_sem,
    p_sem,
):
    a = lax.axis_index("adapter")
    f = lax.axis_index("feature")
    _, count, rows, chunk = flat.shape
    width = part.shape[1]
    mine = lax.rem(a, count)
    base = a - mine
    far = [lax.rem(a + r, na) for r in range(1, na)]
    group = [base + lax.rem(mine + r, count) for r in range(1, count)]
    beside = [lax.rem(f + r, nf) for r in range(1, nf)]

    loads = []
    for w, ref in enumerate((down_ref, up_ref)):
        for c in range(count):
            loads.append(
                pltpu.make_async_copy(
                    ref.at[:, pl.ds(c * chunk, chunk)], flat.at[w, c], load_sem.at[w, c]
                )
            )
    prompt_loads = [
        pltpu.make_async_copy(
            prompt_ref.at[:, pl.ds(c * chunk, chunk)], prompt.at[c], prompt_sem.at[c]
        )
        for c in range(count)
    ]
    for copy in loads + prompt_loads:
        copy.start()

    barrier = pltpu.get_barrier_semaphore()
    for to in far:
        pl.semaphore_signal(barrier, inc=1, device_id=(to, f), device_id_type=MESH)
    for to in beside:
        pl.semaphore_signal(barrier, inc=1, device_id=(a, to), device_id_type=MESH)

    def over_adapter(source, target, sems, r, to):
        return pltpu.make_async_remote_copy(
            src_ref=source,
            dst_ref=target,
            send_sem=sems.at[0, r],
            recv_sem=sems.at[1, r],
            device_id=(to, f),
            device_id_type=MESH,
        )

    def over_feature(source, target, sems, r, to):
        return pltpu.make_async_remote_copy(
            src_ref=source,
            dst_ref=target,
            send_sem=sems.at[0, r],
            recv_sem=sems.at[1, r],
            device_id=(a, to),
            device_id_type=MESH,
        )

    for w, ref in enumerate((init_v_ref, init_u_ref)):
        total = jnp.zeros((rows, width), jnp.float32)
        for c in range(count):
            loads[w * count + c].wait()
            basis = ref[c * chunk : (c + 1) * chunk, :].astype(jnp.bfloat16)
            total += jnp.dot(flat[w, c], basis, preferred_element_type=jnp.float32)
        init_out[w] = total.T.astype(init_out.dtype)
    pl.semaphore_wait(barrier, na - 1 + nf - 1)
    copies = [
        over_feature(init_out, init_in.at[r], init_sem, r, to) for r, to in enumerate(beside)
    ]
    for copy in copies:
        copy.start()
    for copy in copies:
        copy.wait()
    total = init_out[...].astype(jnp.float32)
    for r in range(nf - 1):
        total += init_in[r].astype(jnp.float32)
    factors[...] = total

    weights = weights_ref[...]

    def half(h, last):
        even = 1 - lax.rem(h, 2)
        w = even
        parity = 1 - even
        low = weigh(rank, factors[1 - w], factors[w], weights)
        for c in range(count):
            part[c] = jnp.dot(low, flat[w, c], preferred_element_type=jnp.float32).astype(part.dtype)
        scatter = [
            over_adapter(part.at[lax.rem(to, count)], arrived.at[r], scatter_sem, r, to)
            for r, to in enumerate(far)
        ]
        for copy in scatter:
            copy.start()
        total = part[mine].astype(jnp.float32)
        for r, copy in enumerate(scatter):
            copy.wait_recv()
            total += arrived[r].astype(jnp.float32)
        own = total.astype(numerator.dtype)
        numerator[parity, mine] = own
        gather = [
            over_adapter(numerator.at[parity, mine], numerator.at[parity, mine], gather_sem, r, to)
            for r, to in enumerate(group)
        ]
        for copy in gather:
            copy.start()
        proj = dot_nt(own, flat[w, mine])
        gram = dot_nt(own, own)
        if last:
            hidden = dot_nt(own, prompt[mine])
        for r, copy in enumerate(gather):
            copy.wait_recv()
            c = lax.rem(mine + (count - 1 - r), count)
            piece = numerator[parity, c]
            proj += dot_nt(piece, flat[w, c])
            gram += dot_nt(piece, piece)
            if last:
                hidden += dot_nt(piece, prompt[c])
        proj_out[...] = proj.astype(proj_out.dtype)
        gram_out[...] = fold(gram)
        sends = []
        for r, to in enumerate(beside):
            sends.append(
                over_feature(gram_out, gram_in.at[parity, r], gram_sem.at[parity], r, to)
            )
        for r, to in enumerate(beside):
            sends.append(
                over_feature(proj_out, proj_in.at[parity, r], proj_sem.at[parity], r, to)
            )
        for copy in sends:
            copy.start()
        if last:
            hidden_out[...] = hidden.astype(hidden_out.dtype)
            late = [
                over_feature(hidden_out, hidden_in.at[r], hidden_sem, r, to)
                for r, to in enumerate(beside)
            ]
            for copy in late:
                copy.start()
        for copy in sends[: nf - 1]:
            copy.wait_recv()
        square = gram_out[...]
        for r in range(nf - 1):
            square += gram_in[parity, r]
        inverse = inverse_factor(unfold(square))
        for copy in sends[nf - 1 :]:
            copy.wait_recv()
        total = proj_out[...].astype(jnp.float32)
        for r in range(nf - 1):
            total += proj_in[parity, r].astype(jnp.float32)
        fresh = dot32(inverse, total)
        factors[w] = fresh
        for copy in scatter + gather + sends:
            copy.wait_send()
        if not last:
            return inverse
        return inverse, fresh, late

    inverse_u = lax.fori_loop(
        0,
        2 * SWEEPS - 1,
        lambda h, _: half(h, False),
        jnp.zeros((width, width), jnp.float32),
    )
    all_q[a] = factors[1].astype(all_q.dtype)
    spread_q = [over_adapter(all_q.at[a], all_q.at[a], q_sem, r, to) for r, to in enumerate(far)]
    for copy in spread_q:
        copy.start()
    for c in range(count):
        basis_ref[:, c * chunk : (c + 1) * chunk] = dot32(
            inverse_u, numerator[0, c].astype(jnp.float32)
        ).astype(basis_ref.dtype)
    for copy in prompt_loads:
        copy.wait()
    inverse_v, fresh, late = half(2 * SWEEPS - 1, True)
    all_p[a] = fresh.astype(all_p.dtype)
    spread_p = [over_adapter(all_p.at[a], all_p.at[a], p_sem, r, to) for r, to in enumerate(far)]
    for copy in spread_p:
        copy.start()
    for copy in late:
        copy.wait()
    total = hidden_out[...].astype(jnp.float32)
    for r in range(nf - 1):
        total += hidden_in[r].astype(jnp.float32)
    hidden = dot32(inverse_v, total).astype(jnp.bfloat16)
    for copy in spread_q + spread_p:
        copy.wait()
    blocks = ids_ref.shape[0]
    block = hidden.shape[1] // blocks
    owner = lax.broadcasted_iota(jnp.int32, (1, rows), 1) // rank
    for b in range(blocks):
        at = ids_ref[b]
        device, inside = at // (rows // rank), lax.rem(at, rows // rank)
        chosen_q = jnp.where(owner == inside, all_q[device], 0)
        core = dot_nt(chosen_q, all_p[device]).astype(jnp.bfloat16)
        mixed = jnp.dot(
            core, hidden[:, b * block : (b + 1) * block], preferred_element_type=jnp.float32
        )
        mixed_ref[b * block : (b + 1) * block, :] = mixed.T.astype(mixed_ref.dtype)


def on_device(na, nf, adapter_down, adapter_up, fisher, init_v, init_u, prompt_rows, request_ids):
    count_local, rank, depth = adapter_up.shape
    width = init_v.shape[1]
    rows = count_local * rank
    down = adapter_down.reshape(rows, depth)
    up = adapter_up.reshape(rows, depth)
    weights = jnp.repeat(fisher, rank)[None, :]
    tall = prompt_rows.shape[0]
    count = math.gcd(na, depth // LANES)
    chunk = depth // count
    dma = pltpu.SemaphoreType.DMA
    anywhere = pl.BlockSpec(memory_space=pl.ANY)
    vmem = pl.BlockSpec(memory_space=pltpu.VMEM)
    mixed, basis_u = pl.pallas_call(
        functools.partial(kernel, na, nf, rank),
        out_shape=[
            jax.ShapeDtypeStruct((tall, width), jnp.bfloat16),
            jax.ShapeDtypeStruct((width, depth), jnp.bfloat16),
        ],
        in_specs=[anywhere] * 3 + [vmem] * 3 + [pl.BlockSpec(memory_space=pltpu.SMEM)],
        out_specs=[vmem, vmem],
        scratch_shapes=[
            pltpu.VMEM((2, count, rows, chunk), jnp.bfloat16),
            pltpu.VMEM((count, tall, chunk), jnp.bfloat16),
            pltpu.VMEM((2, width, rows), jnp.float32),
            pltpu.VMEM((count, width, chunk), SEND),
            pltpu.VMEM((na - 1, width, chunk), SEND),
            pltpu.VMEM((2, count, width, chunk), jnp.bfloat16),
            pltpu.VMEM((width, rows), SEND),
            pltpu.VMEM((width // 2, 2 * width), jnp.float32),
            pltpu.VMEM((2, nf - 1, width, rows), SEND),
            pltpu.VMEM((2, nf - 1, width // 2, 2 * width), jnp.float32),
            pltpu.VMEM((2, width, rows), SEND),
            pltpu.VMEM((nf - 1, 2, width, rows), SEND),
            pltpu.VMEM((width, tall), SEND),
            pltpu.VMEM((nf - 1, width, tall), SEND),
            pltpu.VMEM((na, width, rows), jnp.bfloat16),
            pltpu.VMEM((na, width, rows), jnp.bfloat16),
            dma((2, count)),
            dma((count,)),
            dma((2, na - 1)),
            dma((2, count - 1)),
            dma((2, 2, nf - 1)),
            dma((2, 2, nf - 1)),
            dma((2, nf - 1)),
            dma((2, nf - 1)),
            dma((2, na - 1)),
            dma((2, na - 1)),
        ],
        compiler_params=pltpu.CompilerParams(
            vmem_limit_bytes=48 * 2**20, collective_id=0, has_side_effects=True
        ),
    )(down, up, prompt_rows, init_v, init_u, weights, request_ids)
    served = jnp.dot(mixed, basis_u, preferred_element_type=jnp.float32)
    return served.astype(jnp.bfloat16)


def solution(mesh):
    placed = (
        P("adapter", None, "feature"),
        P("adapter", None, "feature"),
        P("adapter"),
        P("feature", None),
        P("feature", None),
        P("adapter", "feature"),
        P("adapter"),
    )
    body = functools.partial(on_device, mesh.shape["adapter"], mesh.shape["feature"])
    return jax.shard_map(
        body, mesh=mesh, in_specs=placed, out_specs=P("adapter", "feature"), check_vma=False
    )
```

```python
import functools
import math

import jax
import jax.numpy as jnp
from jax import lax
from jax.experimental import pallas as pl
from jax.experimental.pallas import tpu as pltpu
from jax.sharding import PartitionSpec as P

SWEEPS = 3
GROUP = 8
LANES = 128
MESH = pl.DeviceIdType.MESH
SUBS = 2
SEND = jnp.bfloat16

highest = lax.Precision.HIGHEST


def dot32(left, right):
    return jnp.dot(left, right, precision=highest, preferred_element_type=jnp.float32)


def dot_nt(left, right):
    return lax.dot_general(
        left, right, (((1,), (1,)), ((), ())), preferred_element_type=jnp.float32
    )


def dot_split(left, right):
    left_high, right_high = left.astype(jnp.bfloat16), right.astype(jnp.bfloat16)
    left_low = (left - left_high.astype(jnp.float32)).astype(jnp.bfloat16)
    right_low = (right - right_high.astype(jnp.float32)).astype(jnp.bfloat16)
    dot = functools.partial(jnp.dot, preferred_element_type=jnp.float32)
    return dot(left_high, right_high) + (dot(left_high, right_low) + dot(left_low, right_high))


def inverse_factor(gram):
    width = gram.shape[0]
    shape = (width, width)
    eye = lax.broadcasted_iota(jnp.int32, shape, 0) == lax.broadcasted_iota(jnp.int32, shape, 1)
    table = jnp.concatenate([gram, eye.astype(jnp.float32)], axis=1)
    blocks = [table[at : at + GROUP] for at in range(0, width, GROUP)]
    full = functools.partial(jnp.broadcast_to, shape=(GROUP, 2 * width))
    inner = lax.broadcasted_iota(jnp.int32, (GROUP, 2 * width), 0)
    result = []
    for b, block in enumerate(blocks):
        at = b * GROUP
        columns = [full(block[:, at + j : at + j + 1]) for j in range(GROUP)]
        entry = [[full(columns[j][i : i + 1]) for j in range(i + 1)] for i in range(GROUP)]
        row = [full(block[i : i + 1]) for i in range(GROUP)]
        inverse = []
        done = None
        for i in range(GROUP):
            inverse.append(1.0 / entry[i][i])
            for j in range(i + 1, GROUP):
                factor = entry[j][i] * inverse[i]
                for q in range(i + 1, j + 1):
                    entry[j][q] = entry[j][q] - factor * entry[q][i]
                row[j] = row[j] - factor * row[i]
            scaled = row[i] / jnp.sqrt(entry[i][i])
            done = scaled if done is None else jnp.where(inner == i, scaled, done)
        result.append(done)
        for c in range(b + 1, len(blocks)):
            columns = [full(blocks[c][:, at + j : at + j + 1]) for j in range(GROUP)]
            new = blocks[c]
            for i in range(GROUP):
                factor = columns[i] * inverse[i]
                for j in range(i + 1, GROUP):
                    columns[j] = columns[j] - factor * entry[j][i]
                new = new - factor * row[i]
            blocks[c] = new
    return jnp.concatenate(result, axis=0)[:, width:]


def weigh(rank, fresh, other, weights):
    total = fresh.shape[1]
    step = 128 if total % 128 == 0 and 128 % rank == 0 else total
    same = (
        lax.broadcasted_iota(jnp.int32, (step, step), 0) // rank
        == lax.broadcasted_iota(jnp.int32, (step, step), 1) // rank
    )
    parts = []
    for at in range(0, total, step):
        piece = fresh[:, at : at + step]
        inner = jnp.where(same, dot_split(piece.T, piece), 0.0)
        parts.append(dot_split(other[:, at : at + step], inner))
    joined = parts[0] if len(parts) == 1 else jnp.concatenate(parts, axis=1)
    return (joined * weights).astype(jnp.bfloat16)


def fold(square):
    half = square.shape[0] // 2
    return jnp.concatenate([square[:half], square[half:]], axis=1)


def unfold(packed):
    width = packed.shape[1] // 2
    return jnp.concatenate([packed[:, :width], packed[:, width:]], axis=0)


def kernel(
    na,
    nf,
    rank,
    down_ref,
    up_ref,
    prompt_ref,
    init_v_ref,
    init_u_ref,
    weights_ref,
    ids_ref,
    mixed_ref,
    basis_ref,
    flat,
    prompt,
    factors,
    part,
    arrived,
    numerator,
    proj_out,
    gram_out,
    proj_in,
    gram_in,
    init_out,
    init_in,
    hidden_out,
    hidden_in,
    all_q,
    all_p,
    inverse_ref,
    load_sem,
    prompt_sem,
    scatter_sem,
    gather_sem,
    proj_sem,
    gram_sem,
    init_sem,
    hidden_sem,
    q_sem,
    p_sem,
):
    a = lax.axis_index("adapter")
    f = lax.axis_index("feature")
    _, count, rows, chunk = flat.shape
    _, subs, width, sub = part.shape
    mine = lax.rem(a, count)
    base = a - mine
    far = [lax.rem(a + r, na) for r in range(1, na)]
    beside = [lax.rem(f + r, nf) for r in range(1, nf)]

    loads = []
    for w, ref in enumerate((down_ref, up_ref)):
        for c in range(count):
            loads.append(
                pltpu.make_async_copy(
                    ref.at[:, pl.ds(c * chunk, chunk)], flat.at[w, c], load_sem.at[w, c]
                )
            )
    prompt_loads = [
        pltpu.make_async_copy(
            prompt_ref.at[:, pl.ds(c * chunk, chunk)], prompt.at[c], prompt_sem.at[c]
        )
        for c in range(count)
    ]
    for copy in loads + prompt_loads:
        copy.start()

    barrier = pltpu.get_barrier_semaphore()
    for to in far:
        pl.semaphore_signal(barrier, inc=1, device_id=(to, f), device_id_type=MESH)
    for to in beside:
        pl.semaphore_signal(barrier, inc=1, device_id=(a, to), device_id_type=MESH)

    def over_adapter(source, target, sems, r, to):
        return pltpu.make_async_remote_copy(
            src_ref=source,
            dst_ref=target,
            send_sem=sems.at[0, r],
            recv_sem=sems.at[1, r],
            device_id=(to, f),
            device_id_type=MESH,
        )

    def over_feature(source, target, sems, r, to):
        return pltpu.make_async_remote_copy(
            src_ref=source,
            dst_ref=target,
            send_sem=sems.at[0, r],
            recv_sem=sems.at[1, r],
            device_id=(a, to),
            device_id_type=MESH,
        )

    for w, ref in enumerate((init_v_ref, init_u_ref)):
        total = jnp.zeros((width, rows), jnp.float32)
        for c in range(count):
            loads[w * count + c].wait()
            basis = ref[:, c * chunk : (c + 1) * chunk].astype(jnp.bfloat16)
            total += dot_nt(basis, flat[w, c])
        init_out[w] = total.astype(init_out.dtype)
    pl.semaphore_wait(barrier, na - 1 + nf - 1)
    copies = [
        over_feature(init_out, init_in.at[r], init_sem, r, to) for r, to in enumerate(beside)
    ]
    for copy in copies:
        copy.start()
    for copy in copies:
        copy.wait()
    total = init_out[...].astype(jnp.float32)
    for r in range(nf - 1):
        total += init_in[r].astype(jnp.float32)
    factors[...] = total

    weights = jnp.zeros((1, rows), jnp.float32)
    lane = lax.broadcasted_iota(jnp.int32, (1, rows), 1) // rank
    for i in range(rows // rank):
        weights = jnp.where(lane == i, weights_ref[i], weights)

    slots = [(r, q) for q in range(na // count) for r in near(count) if r or q]

    def to_device(r, q):
        return lax.rem(lax.rem(base + q * count, na) + lax.rem(mine + r, count), na)

    def half(h, last):
        w = 1 - lax.rem(h, 2)
        parity = 1 - w
        low = weigh(rank, factors[1 - w], factors[w], weights)
        scatter = [[] for _ in range(subs)]
        for r in near(count):
            c = lax.rem(mine + r, count)
            piece = jnp.dot(low, flat[w, c], preferred_element_type=jnp.float32).astype(part.dtype)
            for s in range(subs):
                part[c, s] = piece[:, s * sub : (s + 1) * sub]
            for q in range(na // count):
                if r or q:
                    at = q * count + r - 1
                    for s in range(subs):
                        copy = over_adapter(
                            part.at[c, s],
                            arrived.at[at, s],
                            scatter_sem.at[s],
                            at,
                            to_device(r, q),
                        )
                        scatter[s].append((at, copy))
                        if s == 0:
                            copy.start()
        for s in range(1, subs):
            for _, copy in scatter[s]:
                copy.start()
        if last:
            for c in range(count):
                for s in range(subs):
                    at = c * chunk + s * sub
                    basis_ref[:, at : at + sub] = dot_split(
                        inverse_ref[...], numerator[0, c, s].astype(jnp.float32)
                    ).astype(basis_ref.dtype)
            for copy in prompt_loads:
                copy.wait()
        gather = [[] for _ in range(subs)]
        proj = jnp.zeros((width, rows), jnp.float32)
        gram = jnp.zeros((width, width), jnp.float32)
        hidden = jnp.zeros(hidden_out.shape, jnp.float32) if last else None

        def add(c, s, piece, proj, gram, hidden):
            lanes = slice(s * sub, (s + 1) * sub)
            gram += dot_nt(piece, piece)
            proj += dot_nt(piece, flat[w, c, :, lanes])
            if last:
                hidden += dot_nt(piece, prompt[c, :, lanes])
            return proj, gram, hidden

        for s in range(subs):
            total = part[mine, s].astype(jnp.float32)
            for at, copy in scatter[s]:
                copy.wait_recv()
                total += arrived[at, s].astype(jnp.float32)
            own = total.astype(numerator.dtype)
            numerator[parity, mine, s] = own
            for r in near(count)[1:]:
                copy = over_adapter(
                    numerator.at[parity, mine, s],
                    numerator.at[parity, mine, s],
                    gather_sem.at[s],
                    r - 1,
                    base + lax.rem(mine + r, count),
                )
                copy.start()
                gather[s].append((r, copy))
            proj, gram, hidden = add(mine, s, own, proj, gram, hidden)
        for s in range(subs):
            for r, copy in gather[s]:
                copy.wait_recv()
                c = lax.rem(mine + count - r, count)
                proj, gram, hidden = add(c, s, numerator[parity, c, s], proj, gram, hidden)
        gram_out[...] = fold(gram)
        gram_sends = [
            over_feature(gram_out, gram_in.at[parity, r], gram_sem.at[parity], r, to)
            for r, to in enumerate(beside)
        ]
        for copy in gram_sends:
            copy.start()
        proj_out[...] = proj.astype(proj_out.dtype)
        proj_sends = [
            over_feature(proj_out, proj_in.at[parity, r], proj_sem.at[parity], r, to)
            for r, to in enumerate(beside)
        ]
        for copy in proj_sends:
            copy.start()
        late = []
        if last:
            hidden_out[...] = hidden.astype(hidden_out.dtype)
            late = [
                over_feature(hidden_out, hidden_in.at[r], hidden_sem, r, to)
                for r, to in enumerate(beside)
            ]
            for copy in late:
                copy.start()
            all_q[a] = factors[1].astype(all_q.dtype)
            late += spread(all_q, q_sem)
            for copy in proj_sends:
                copy.wait_recv()
            total = proj_out[...].astype(jnp.float32)
            for r in range(nf - 1):
                total += proj_in[parity, r].astype(jnp.float32)
            all_p[a] = total.astype(all_p.dtype)
            late += spread(all_p, p_sem)
        for copy in gram_sends:
            copy.wait_recv()
        square = gram_out[...]
        for r in range(nf - 1):
            square += gram_in[parity, r]
        inverse = inverse_factor(unfold(square))
        inverse_ref[...] = inverse
        if not last:
            for copy in proj_sends:
                copy.wait_recv()
            total = proj_out[...].astype(jnp.float32)
            for r in range(nf - 1):
                total += proj_in[parity, r].astype(jnp.float32)
            factors[w] = dot32(inverse, total)
        for s in range(subs):
            for _, copy in scatter[s] + gather[s]:
                copy.wait_send()
        for copy in gram_sends + proj_sends:
            copy.wait_send()
        return late

    def spread(table, sems):
        copies = [
            over_adapter(table.at[a], table.at[a], sems, q * count + r - 1, to_device(r, q))
            for r, q in slots
        ]
        for copy in copies:
            copy.start()
        return copies

    def step(h, carry):
        half(h, False)
        return carry

    lax.fori_loop(0, 2 * SWEEPS - 1, step, 0)
    late = half(2 * SWEEPS - 1, True)
    inverse = inverse_ref[...]
    for copy in late[: nf - 1]:
        copy.wait()
    total = hidden_out[...].astype(jnp.float32)
    for r in range(nf - 1):
        total += hidden_in[r].astype(jnp.float32)
    hidden = dot_split(inverse, total).astype(jnp.bfloat16)
    blocks = ids_ref.shape[0]
    block = hidden.shape[1] // blocks
    per = rows // rank
    owners, picks = [], []
    shape = (rows, blocks * rank)
    row, column = lax.broadcasted_iota(jnp.int32, shape, 0), lax.broadcasted_iota(jnp.int32, shape, 1)
    for b in range(blocks):
        at = ids_ref[b]
        owners.append(at // per)
        wanted = (row == column - b * rank + lax.rem(at, per) * rank) & (column // rank == b)
        picks.append(jnp.where(wanted, 1.0, 0.0).astype(jnp.bfloat16))

    def pick(table):
        return sum(
            jnp.dot(table[owners[b]], picks[b], preferred_element_type=jnp.float32)
            for b in range(blocks)
        )

    for copy in late[nf - 1 : nf - 1 + na - 1]:
        copy.wait()
    chosen_q = pick(all_q).astype(jnp.bfloat16)
    for copy in late[nf - 1 + na - 1 :]:
        copy.wait()
    chosen_p = dot32(inverse, pick(all_p)).astype(jnp.bfloat16)
    owner = lax.broadcasted_iota(jnp.int32, (1, blocks * rank), 1) // rank
    for b in range(blocks):
        core = dot_nt(jnp.where(owner == b, chosen_q, 0), chosen_p).astype(jnp.bfloat16)
        mixed = jnp.dot(
            core, hidden[:, b * block : (b + 1) * block], preferred_element_type=jnp.float32
        )
        mixed_ref[b * block : (b + 1) * block, :] = mixed.T.astype(mixed_ref.dtype)


def near(count):
    return sorted(range(count), key=lambda r: (min(r, count - r), r))


def on_device(na, nf, adapter_down, adapter_up, fisher, init_v, init_u, prompt_rows, request_ids):
    count_local, rank, depth = adapter_up.shape
    width = init_v.shape[1]
    rows = count_local * rank
    down = adapter_down.reshape(rows, depth)
    up = adapter_up.reshape(rows, depth)
    tall = prompt_rows.shape[0]
    count = math.gcd(na, depth // LANES)
    chunk = depth // count
    subs = SUBS if chunk % (SUBS * LANES) == 0 else 1
    sub = chunk // subs
    dma = pltpu.SemaphoreType.DMA
    anywhere = pl.BlockSpec(memory_space=pl.ANY)
    vmem = pl.BlockSpec(memory_space=pltpu.VMEM)
    mixed, basis_u = pl.pallas_call(
        functools.partial(kernel, na, nf, rank),
        out_shape=[
            jax.ShapeDtypeStruct((tall, width), jnp.bfloat16),
            jax.ShapeDtypeStruct((width, depth), jnp.bfloat16),
        ],
        in_specs=[anywhere] * 3 + [vmem] * 2 + [pl.BlockSpec(memory_space=pltpu.SMEM)] * 2,
        out_specs=[vmem, vmem],
        scratch_shapes=[
            pltpu.VMEM((2, count, rows, chunk), jnp.bfloat16),
            pltpu.VMEM((count, tall, chunk), jnp.bfloat16),
            pltpu.VMEM((2, width, rows), jnp.float32),
            pltpu.VMEM((count, subs, width, sub), SEND),
            pltpu.VMEM((na - 1, subs, width, sub), SEND),
            pltpu.VMEM((2, count, subs, width, sub), jnp.bfloat16),
            pltpu.VMEM((width, rows), SEND),
            pltpu.VMEM((width // 2, 2 * width), jnp.float32),
            pltpu.VMEM((2, nf - 1, width, rows), SEND),
            pltpu.VMEM((2, nf - 1, width // 2, 2 * width), jnp.float32),
            pltpu.VMEM((2, width, rows), SEND),
            pltpu.VMEM((nf - 1, 2, width, rows), SEND),
            pltpu.VMEM((width, tall), SEND),
            pltpu.VMEM((nf - 1, width, tall), SEND),
            pltpu.VMEM((na, width, rows), jnp.bfloat16),
            pltpu.VMEM((na, width, rows), jnp.bfloat16),
            pltpu.VMEM((width, width), jnp.float32),
            dma((2, count)),
            dma((count,)),
            dma((subs, 2, na - 1)),
            dma((subs, 2, count - 1)),
            dma((2, 2, nf - 1)),
            dma((2, 2, nf - 1)),
            dma((2, nf - 1)),
            dma((2, nf - 1)),
            dma((2, na - 1)),
            dma((2, na - 1)),
        ],
        compiler_params=pltpu.CompilerParams(
            vmem_limit_bytes=63 * 2**20, collective_id=0, has_side_effects=True
        ),
    )(down, up, prompt_rows, init_v.T, init_u.T, fisher, request_ids)
    served = jnp.dot(mixed, basis_u, preferred_element_type=jnp.float32)
    return served.astype(jnp.bfloat16)


def solution(mesh):
    placed = (
        P("adapter", None, "feature"),
        P("adapter", None, "feature"),
        P("adapter"),
        P("feature", None),
        P("feature", None),
        P("adapter", "feature"),
        P("adapter"),
    )
    body = functools.partial(on_device, mesh.shape["adapter"], mesh.shape["feature"])
    return jax.shard_map(
        body, mesh=mesh, in_specs=placed, out_specs=P("adapter", "feature"), check_vma=False
    )
```

```python
import functools
import math

import jax
import jax.numpy as jnp
from jax import lax
from jax.experimental import pallas as pl
from jax.experimental.pallas import tpu as pltpu
from jax.sharding import PartitionSpec as P

SWEEPS = 3
GROUP = 8
LANES = 128
VMEM_BYTES = int(53.1 * 2**20)
MESH = pl.DeviceIdType.MESH
SUBS = 2
SEND = jnp.bfloat16

def dot_nt(left, right):
    return lax.dot_general(
        left, right, (((1,), (1,)), ((), ())), preferred_element_type=jnp.float32
    )


def dot_split(left, right):
    left_high, left_low = halves(left)
    right_high, right_low = halves(right)
    dot = functools.partial(jnp.dot, preferred_element_type=jnp.float32)
    return dot(left_high, right_high) + (dot(left_high, right_low) + dot(left_low, right_high))


def inverse_factor(gram):
    width = gram.shape[0]
    shape = (width, width)
    eye = lax.broadcasted_iota(jnp.int32, shape, 0) == lax.broadcasted_iota(jnp.int32, shape, 1)
    table = jnp.concatenate([gram, eye.astype(jnp.float32)], axis=1)
    blocks = [table[at : at + GROUP] for at in range(0, width, GROUP)]
    full = functools.partial(jnp.broadcast_to, shape=(GROUP, 2 * width))
    inner = lax.broadcasted_iota(jnp.int32, (GROUP, 2 * width), 0)
    result = []
    for b, block in enumerate(blocks):
        at = b * GROUP
        columns = [full(block[:, at + j : at + j + 1]) for j in range(GROUP)]
        entry = [[full(columns[j][i : i + 1]) for j in range(i + 1)] for i in range(GROUP)]
        row = [full(block[i : i + 1]) for i in range(GROUP)]
        inverse = []
        done = None
        for i in range(GROUP):
            inverse.append(1.0 / entry[i][i])
            for j in range(i + 1, GROUP):
                factor = entry[j][i] * inverse[i]
                for q in range(i + 1, j + 1):
                    entry[j][q] = entry[j][q] - factor * entry[q][i]
                row[j] = row[j] - factor * row[i]
            scaled = row[i] / jnp.sqrt(entry[i][i])
            done = scaled if done is None else jnp.where(inner == i, scaled, done)
        result.append(done)
        for c in range(b + 1, len(blocks)):
            columns = [full(blocks[c][:, at + j : at + j + 1]) for j in range(GROUP)]
            new = blocks[c]
            for i in range(GROUP):
                factor = columns[i] * inverse[i]
                for j in range(i + 1, GROUP):
                    columns[j] = columns[j] - factor * entry[j][i]
                new = new - factor * row[i]
            blocks[c] = new
    return jnp.concatenate(result, axis=0)[:, width:]


def halves(full):
    high = full.astype(jnp.bfloat16)
    return high, (full - high.astype(jnp.float32)).astype(jnp.bfloat16)


def weigh(rank, fresh, other, weights):
    total = fresh.shape[1]
    step = 128 if total % 128 == 0 and 128 % rank == 0 else total
    same = (
        lax.broadcasted_iota(jnp.int32, (step, step), 0) // rank
        == lax.broadcasted_iota(jnp.int32, (step, step), 1) // rank
    )
    dot = functools.partial(jnp.dot, preferred_element_type=jnp.float32)
    parts = []
    for at in range(0, total, step):
        high, low = halves(fresh[:, at : at + step])
        inner = lax.dot_general(
            jnp.concatenate([high, high, low], axis=0),
            jnp.concatenate([high, low, high], axis=0),
            (((0,), (0,)), ((), ())),
            preferred_element_type=jnp.float32,
        )
        inner_high, inner_low = halves(jnp.where(same, inner, 0.0))
        other_high, other_low = halves(other[:, at : at + step])
        parts.append(
            dot(
                jnp.concatenate([other_high, other_high], axis=1),
                jnp.concatenate([inner_high, inner_low], axis=0),
            )
            + dot(other_low, inner_high)
        )
    joined = parts[0] if len(parts) == 1 else jnp.concatenate(parts, axis=1)
    return (joined * weights).astype(jnp.bfloat16)


def fold(square):
    half = square.shape[0] // 2
    return jnp.concatenate([square[:half], square[half:]], axis=1)


def unfold(packed):
    width = packed.shape[1] // 2
    return jnp.concatenate([packed[:, :width], packed[:, width:]], axis=0)


def kernel(
    na,
    nf,
    rank,
    down_ref,
    up_ref,
    prompt_ref,
    init_v_ref,
    init_u_ref,
    weights_ref,
    ids_ref,
    mixed_ref,
    basis_ref,
    flat,
    prompt,
    factors,
    part,
    arrived,
    numerator,
    proj_out,
    gram_out,
    proj_in,
    gram_in,
    init_out,
    init_in,
    hidden_out,
    hidden_in,
    starts,
    asked,
    picks,
    q_out,
    q_in,
    p_out,
    p_in,
    inverse_ref,
    start_sem,
    load_sem,
    prompt_sem,
    asked_sem,
    scatter_sem,
    gather_sem,
    proj_sem,
    gram_sem,
    init_sem,
    hidden_sem,
    q_sem,
    p_sem,
):
    a = lax.axis_index("adapter")
    f = lax.axis_index("feature")
    _, count, rows, chunk = flat.shape
    _, subs, width, sub = part.shape
    mine = lax.rem(a, count)
    base = a - mine
    far = [lax.rem(a + r, na) for r in range(1, na)]
    beside = [lax.rem(f + r, nf) for r in range(1, nf)]

    loads = []
    for w, (start_ref, ref) in enumerate(((init_v_ref, down_ref), (init_u_ref, up_ref))):
        loads.append(
            [pltpu.make_async_copy(start_ref, starts.at[w], start_sem.at[w])]
            + [
                pltpu.make_async_copy(
                    ref.at[:, pl.ds(c * chunk, chunk)], flat.at[w, c], load_sem.at[w, c]
                )
                for c in range(count)
            ]
        )
        for copy in loads[w]:
            copy.start()
    prompt_loads = [
        pltpu.make_async_copy(
            prompt_ref.at[:, pl.ds(c * chunk, chunk)], prompt.at[c], prompt_sem.at[c]
        )
        for c in range(count)
    ]

    barrier = pltpu.get_barrier_semaphore()
    for to in far:
        pl.semaphore_signal(barrier, inc=1, device_id=(to, f), device_id_type=MESH)
    for to in beside:
        pl.semaphore_signal(barrier, inc=1, device_id=(a, to), device_id_type=MESH)

    def over_adapter(source, target, sems, r, to):
        return pltpu.make_async_remote_copy(
            src_ref=source,
            dst_ref=target,
            send_sem=sems.at[0, r],
            recv_sem=sems.at[1, r],
            device_id=(to, f),
            device_id_type=MESH,
        )

    def over_feature(source, target, sems, r, to):
        return pltpu.make_async_remote_copy(
            src_ref=source,
            dst_ref=target,
            send_sem=sems.at[0, r],
            recv_sem=sems.at[1, r],
            device_id=(a, to),
            device_id_type=MESH,
        )

    slots = [(r, q) for q in range(na // count) for r in offsets(count) if r or q]

    def slot_of(r, q):
        return q * count + r - 1

    def to_device(r, q):
        return lax.rem(lax.rem(base + q * count, na) + lax.rem(mine + r, count), na)

    blocks = ids_ref.shape[0]
    wide = blocks * rank
    column = lax.broadcasted_iota(jnp.int32, asked.shape[1:], 1) // rank
    wanted = jnp.zeros(asked.shape[1:], jnp.int32)
    for i in range(blocks):
        wanted = jnp.where(column == i, ids_ref[i], wanted)
    asked[a] = wanted

    first_sends = []
    for w in range(2):
        total = jnp.zeros((width, rows), jnp.float32)
        loads[w][0].wait()
        for c in range(count):
            loads[w][1 + c].wait()
            basis = starts[w, :, c * chunk : (c + 1) * chunk].astype(jnp.bfloat16)
            total += dot_nt(basis, flat[w, c])
        init_out[w] = total.astype(init_out.dtype)
        if w == 0:
            pl.semaphore_wait(barrier, na - 1 + nf - 1)
        copies = [
            over_feature(init_out.at[w], init_in.at[r, w], init_sem.at[w], r, to)
            for r, to in enumerate(beside)
        ]
        for copy in copies:
            copy.start()
        first_sends += copies
    asked_sends = [
        over_adapter(asked.at[a], asked.at[a], asked_sem, slot_of(r, q), to_device(r, q))
        for r, q in slots
    ]
    for copy in asked_sends + prompt_loads:
        copy.start()
    for copy in first_sends:
        copy.wait()
    total = init_out[...].astype(jnp.float32)
    for r in range(nf - 1):
        total += init_in[r].astype(jnp.float32)
    factors[...] = total

    weights = jnp.zeros((1, rows), jnp.float32)
    lane = lax.broadcasted_iota(jnp.int32, (1, rows), 1) // rank
    for i in range(rows // rank):
        weights = jnp.where(lane == i, weights_ref[i], weights)

    def half(h, last):
        w = 1 - lax.rem(h, 2)
        parity = 1 - w
        low = weigh(rank, factors[1 - w], factors[w], weights)
        scatter = [[] for _ in range(subs)]
        for r in offsets(count):
            c = lax.rem(mine + r, count)
            piece = jnp.dot(low, flat[w, c], preferred_element_type=jnp.float32).astype(part.dtype)
            for s in range(subs):
                part[c, s] = piece[:, s * sub : (s + 1) * sub]
            for q in range(na // count):
                if r or q:
                    at = slot_of(r, q)
                    for s in range(subs):
                        copy = over_adapter(
                            part.at[c, s],
                            arrived.at[at, s],
                            scatter_sem.at[s],
                            at,
                            to_device(r, q),
                        )
                        scatter[s].append((at, copy))
                        if s == 0:
                            copy.start()
        for s in range(1, subs):
            for _, copy in scatter[s]:
                copy.start()
        if last:
            for c in range(count):
                for s in range(subs):
                    at = c * chunk + s * sub
                    basis_ref[:, at : at + sub] = dot_split(
                        inverse_ref[...], numerator[0, c, s].astype(jnp.float32)
                    ).astype(basis_ref.dtype)
            choose()
            late = spread(factors[1], q_out, q_in, q_sem)
            for copy in prompt_loads:
                copy.wait()
        gather = [[] for _ in range(subs)]
        proj = jnp.zeros((width, rows), jnp.float32)
        gram = jnp.zeros((width, width), jnp.float32)

        def add(c, s, piece, proj, gram):
            lanes = slice(s * sub, (s + 1) * sub)
            gram += dot_nt(piece, piece)
            proj += dot_nt(piece, flat[w, c, :, lanes])
            return proj, gram

        for s in range(subs):
            total = part[mine, s].astype(jnp.float32)
            for at, copy in scatter[s]:
                copy.wait_recv()
                total += arrived[at, s].astype(jnp.float32)
            own = total.astype(numerator.dtype)
            numerator[parity, mine, s] = own
            for r in offsets(count)[1:]:
                copy = over_adapter(
                    numerator.at[parity, mine, s],
                    numerator.at[parity, mine, s],
                    gather_sem.at[s],
                    r - 1,
                    base + lax.rem(mine + r, count),
                )
                copy.start()
                gather[s].append((r, copy))
            proj, gram = add(mine, s, own, proj, gram)
        for s in range(subs):
            for r, copy in gather[s]:
                copy.wait_recv()
                c = lax.rem(mine + count - r, count)
                proj, gram = add(c, s, numerator[parity, c, s], proj, gram)
        gram_out[...] = fold(gram)
        gram_sends = [
            over_feature(gram_out, gram_in.at[parity, r], gram_sem.at[parity], r, to)
            for r, to in enumerate(beside)
        ]
        for copy in gram_sends:
            copy.start()
        proj_out[...] = proj.astype(proj_out.dtype)
        proj_sends = [
            over_feature(proj_out, proj_in.at[parity, r], proj_sem.at[parity], r, to)
            for r, to in enumerate(beside)
        ]
        for copy in proj_sends:
            copy.start()
        if last:
            hidden = jnp.zeros(hidden_out.shape, jnp.float32)
            for c in range(count):
                for s in range(subs):
                    lanes = slice(s * sub, (s + 1) * sub)
                    hidden += dot_nt(numerator[parity, c, s], prompt[c, :, lanes])
            hidden_out[...] = hidden.astype(hidden_out.dtype)
            hidden_sends = [
                over_feature(hidden_out, hidden_in.at[r], hidden_sem, r, to)
                for r, to in enumerate(beside)
            ]
            for copy in hidden_sends:
                copy.start()
            for copy in proj_sends:
                copy.wait_recv()
            total = proj_out[...].astype(jnp.float32)
            for r in range(nf - 1):
                total += proj_in[parity, r].astype(jnp.float32)
            late = hidden_sends + late + spread(total, p_out, p_in, p_sem)
        for copy in gram_sends:
            copy.wait_recv()
        square = gram_out[...]
        for r in range(nf - 1):
            square += gram_in[parity, r]
        inverse = inverse_factor(unfold(square))
        inverse_ref[...] = inverse
        if not last:
            for copy in proj_sends:
                copy.wait_recv()
            total = proj_out[...].astype(jnp.float32)
            for r in range(nf - 1):
                total += proj_in[parity, r].astype(jnp.float32)
            factors[w] = dot_split(inverse, total)
        for s in range(subs):
            for _, copy in scatter[s] + gather[s]:
                copy.wait_send()
        for copy in gram_sends + proj_sends:
            copy.wait_send()
        return late if last else None

    def choose():
        for copy in asked_sends:
            copy.wait()
        shape = (rows, wide)
        row = lax.broadcasted_iota(jnp.int32, shape, 0)
        inside = lax.rem(row, rank) == lax.rem(lax.broadcasted_iota(jnp.int32, shape, 1), rank)
        number = a * (rows // rank) + row // rank
        for r, q in [(0, 0)] + slots:
            hit = inside & (number == asked[to_device(r, q), :1, :wide])
            picks[slot_of(r, q) + 1] = jnp.where(hit, 1.0, 0.0).astype(picks.dtype)

    def spread(table, out, into, sems):
        low = table.astype(jnp.bfloat16)
        copies = []
        for r, q in slots + [(0, 0)]:
            at = slot_of(r, q)
            piece = jnp.dot(low, picks[at + 1], preferred_element_type=jnp.float32)
            out[at + 1] = fold(piece).astype(out.dtype)
            if r or q:
                copies.append(over_adapter(out.at[at + 1], into.at[at], sems, at, to_device(r, q)))
                copies[-1].start()
        return copies

    def gathered(out, into):
        total = out[0].astype(jnp.float32)
        for r in range(na - 1):
            total += into[r].astype(jnp.float32)
        return unfold(total)

    def step(h, carry):
        half(h, False)
        return carry

    lax.fori_loop(0, 2 * SWEEPS - 1, step, 0)
    late = half(2 * SWEEPS - 1, True)
    inverse = inverse_ref[...]
    for copy in late[: nf - 1]:
        copy.wait()
    total = hidden_out[...].astype(jnp.float32)
    for r in range(nf - 1):
        total += hidden_in[r].astype(jnp.float32)
    hidden = dot_split(inverse, total).T.astype(jnp.bfloat16)
    for copy in late[nf - 1 : nf - 1 + na - 1]:
        copy.wait()
    chosen_q = gathered(q_out, q_in).astype(jnp.bfloat16)
    owner = lax.broadcasted_iota(jnp.int32, (1, wide), 1) // rank
    for copy in late[nf - 1 + na - 1 :]:
        copy.wait()
    chosen_p = dot_split(inverse, gathered(p_out, p_in)).astype(jnp.bfloat16)
    block = hidden.shape[0] // blocks
    for i in range(blocks):
        core = dot_nt(jnp.where(owner == i, chosen_q, 0), chosen_p).astype(jnp.bfloat16)
        lines = slice(i * block, (i + 1) * block)
        mixed_ref[lines, :] = dot_nt(hidden[lines], core).astype(mixed_ref.dtype)


def offsets(count):
    return [0] + sorted(range(1, count), key=lambda r: (-min(r, count - r), r))


def on_device(na, nf, adapter_down, adapter_up, fisher, init_v, init_u, prompt_rows, request_ids):
    count_local, rank, depth = adapter_up.shape
    width = init_v.shape[1]
    rows = count_local * rank
    down = adapter_down.reshape(rows, depth)
    up = adapter_up.reshape(rows, depth)
    tall, blocks = prompt_rows.shape[0], request_ids.shape[0]
    count = math.gcd(na, depth // LANES)
    chunk = depth // count
    subs = SUBS if chunk % (SUBS * LANES) == 0 else 1
    sub = chunk // subs
    dma = pltpu.SemaphoreType.DMA
    anywhere = pl.BlockSpec(memory_space=pl.ANY)
    vmem = pl.BlockSpec(memory_space=pltpu.VMEM)
    mixed, basis_u = pl.pallas_call(
        functools.partial(kernel, na, nf, rank),
        out_shape=[
            jax.ShapeDtypeStruct((tall, width), jnp.bfloat16),
            jax.ShapeDtypeStruct((width, depth), jnp.bfloat16),
        ],
        in_specs=[anywhere] * 5 + [pl.BlockSpec(memory_space=pltpu.SMEM)] * 2,
        out_specs=[vmem, vmem],
        scratch_shapes=[
            pltpu.VMEM((2, count, rows, chunk), jnp.bfloat16),
            pltpu.VMEM((count, tall, chunk), jnp.bfloat16),
            pltpu.VMEM((2, width, rows), jnp.float32),
            pltpu.VMEM((count, subs, width, sub), SEND),
            pltpu.VMEM((na - 1, subs, width, sub), SEND),
            pltpu.VMEM((2, count, subs, width, sub), jnp.bfloat16),
            pltpu.VMEM((width, rows), SEND),
            pltpu.VMEM((width // 2, 2 * width), jnp.float32),
            pltpu.VMEM((2, nf - 1, width, rows), SEND),
            pltpu.VMEM((2, nf - 1, width // 2, 2 * width), jnp.float32),
            pltpu.VMEM((2, width, rows), SEND),
            pltpu.VMEM((nf - 1, 2, width, rows), SEND),
            pltpu.VMEM((width, tall), SEND),
            pltpu.VMEM((nf - 1, width, tall), SEND),
            pltpu.VMEM((2, width, depth), jnp.float32),
            pltpu.VMEM((na, 8, -(-blocks * rank // LANES) * LANES), jnp.int32),
            pltpu.VMEM((na, rows, blocks * rank), jnp.bfloat16),
            pltpu.VMEM((na, width // 2, 2 * blocks * rank), jnp.bfloat16),
            pltpu.VMEM((na - 1, width // 2, 2 * blocks * rank), jnp.bfloat16),
            pltpu.VMEM((na, width // 2, 2 * blocks * rank), jnp.bfloat16),
            pltpu.VMEM((na - 1, width // 2, 2 * blocks * rank), jnp.bfloat16),
            pltpu.VMEM((width, width), jnp.float32),
            dma((2,)),
            dma((2, count)),
            dma((count,)),
            dma((2, na - 1)),
            dma((subs, 2, na - 1)),
            dma((subs, 2, count - 1)),
            dma((2, 2, nf - 1)),
            dma((2, 2, nf - 1)),
            dma((2, 2, nf - 1)),
            dma((2, nf - 1)),
            dma((2, na - 1)),
            dma((2, na - 1)),
        ],
        compiler_params=pltpu.CompilerParams(
            vmem_limit_bytes=VMEM_BYTES, collective_id=0, has_side_effects=True
        ),
    )(down, up, prompt_rows, init_v.T, init_u.T, fisher, request_ids)
    served = jnp.dot(mixed, basis_u, preferred_element_type=jnp.float32)
    return served.astype(jnp.bfloat16)


def solution(mesh):
    placed = (
        P("adapter", None, "feature"),
        P("adapter", None, "feature"),
        P("adapter"),
        P("feature", None),
        P("feature", None),
        P("adapter", "feature"),
        P("adapter"),
    )
    body = functools.partial(on_device, mesh.shape["adapter"], mesh.shape["feature"])
    return jax.shard_map(
        body, mesh=mesh, in_specs=placed, out_specs=P("adapter", "feature"), check_vma=False
    )
```
